32 devices in a mesh: gx: 4 (over z), gy: 4 (over y, core), col: 2 (over x).
Axes of the slice: x: 2, y: 2, z: 4, core: 2. Of those that a mesh axis runs over, the one named last changes fastest.
Arguments:
- sources: float32 [4, 4, 2, 128, 1152], P('gx', 'gy', None, 'col'), may hold values from -100 to 100
- impedance: bfloat16 [4, 4, 2, 1152, 1152], P('gx', 'gy'), may hold values from -0.09375 to 0.09375
- pair_maps: bfloat16 [4, 4, 2, 2, 384, 384], P('gx', 'gy'), may hold values from -0.21875 to 0.21875
- lead_side: int32 [4, 4, 2], P('gx', 'gy'), may hold values from 0 to 1
- coarse_basis: float32 [4, 4, 32, 2, 1152], P('gx', 'gy'), may hold values from -0.125 to 0.125
- coarse_inverse: float32 [512, 512], P(('gx', 'gy', 'col')), may hold values from -0.6 to 0.6
Outputs:
- solution_traces: float32 [4, 4, 2, 128, 1152], P('gx', 'gy', None, 'col')
The draws below stay inside these ranges and needn't reach their ends.
Inputs may be any that keep to these rules, and one draw needn't show every extreme that they name: `lead_side`: entries of interfaces beyond the last subdomain along a dimension are read by no step.
All inputs are finite; a program needn't handle non-finite values.
Results may differ from the reference program's by a relative error of at most 0.0039.
Values may be sent and summed in bfloat16 or wider, within the bound.
No kernel may reach another device: no remote copies, remote signals or barrier semaphores. Data moves between devices by JAX's collectives and lax.ppermute only.
A program may use at most 64 MiB of HBM per device.

```python
import math
import jax
import jax.numpy as jnp
from jax import lax

FACE = 192
CPS = 32
ITERS = 2
TRACE = 1152
PAIR = 384
SUB_X = 4
SUB_Y = 4
SRC = 128
COARSE = 512


def draw_sources(key, part):
    subkeys = jax.random.split(jax.random.fold_in(key, 17), 3)
    array_shape = (SUB_X, SUB_Y, 2, SRC, TRACE)
    first_pos = jnp.arange(SUB_X, dtype=jnp.float32) / max(SUB_X - 1, 1)
    second_pos = jnp.arange(SUB_Y, dtype=jnp.float32) / max(SUB_Y - 1, 1)
    growth = 3.0
    entries = jax.random.truncated_normal(subkeys[0], -4.0, 4.0, array_shape, jnp.float32)
    ramp_values = growth ** (first_pos[:, None] + second_pos[None, :] - 1.0)
    col_scale = jnp.exp(jax.random.uniform(subkeys[2], (SUB_X, SUB_Y, 1, 1, TRACE), jnp.float32, math.log(0.5), math.log(2.0)))
    return entries * ramp_values[:, :, None, None, None] * col_scale


def touch_ends(result, rng, low, top_value):
    shape = result.shape
    index_at = [jax.random.randint(jax.random.fold_in(rng, axis), (), 0, shape[axis]) for axis in range(len(shape))]
    result = result.at[tuple(index_at)].set(low)
    longest = shape.index(max(shape))
    index_at[longest] = (index_at[longest] + 1) % shape[longest]
    return result.at[tuple(index_at)].set(top_value)


def steps_of(own_key, extent, shards, smallest, high):
    loudness = 1.0
    for dim, blocks in shards:
        draws = jax.random.uniform(jax.random.fold_in(jax.random.fold_in(own_key, 6), dim), (blocks,), jnp.float32, smallest / len(shards), high / len(shards))
        loudness = loudness * jnp.repeat(jnp.exp(draws), extent[dim] // blocks).reshape((-1,) + (1,) * (len(extent) - 1 - dim))
    return loudness


def centred(rng, extent, deviation, most, cuts=(), kind=jnp.bfloat16):
    array = jax.random.normal(rng, extent, jnp.float32) * deviation
    if len(cuts) > 0:
        array = steps_of(rng, extent, cuts, -0.22, 0.18) * array
    return jnp.clip(array, min=-most, max=most).astype(kind)


def setup_inputs(seed: int = 0) -> dict:
    splits = jax.random.split(jax.random.key(seed), 7)
    return {
        "sources": draw_sources(jax.random.fold_in(splits[6], 71), 0),
        "impedance": centred(splits[1], (SUB_X, SUB_Y, 2, TRACE, TRACE), (4 * TRACE) ** -0.5, 0.09375, ((0, 4), (1, 4))),
        "pair_maps": centred(splits[2], (SUB_X, SUB_Y, 2, 2, PAIR, PAIR), (4 * FACE) ** -0.5, 0.21875, ((0, 4), (1, 4))),
        "lead_side": touch_ends(jax.random.randint(splits[3], (SUB_X, SUB_Y, 2), 0, 2), jax.random.fold_in(splits[3], 1), 0, 1).astype(jnp.int32),
        "coarse_basis": centred(splits[4], (SUB_X, SUB_Y, CPS, 2, TRACE), (2 * TRACE) ** -0.5, 0.125, ((0, 4), (1, 4)), jnp.float32),
        "coarse_inverse": centred(splits[5], (COARSE, COARSE), 0.1, 0.6, ((0, 32),), jnp.float32),
    }


STEP_RATIO = 0.4

def complex_apply(traces, real_part, imag_part):
    first_part = jnp.einsum('...csn,...nm->...csm', traces, real_part, precision=lax.Precision.HIGHEST)
    second_part = jnp.einsum('...csn,...nm->...csm', traces, imag_part, precision=lax.Precision.HIGHEST)
    return jnp.stack([first_part[..., 0, :, :] - second_part[..., 1, :, :], second_part[..., 0, :, :] + first_part[..., 1, :, :]], axis=-3)

def subdomain_map(inputs):
    rounded, map_pair, drive_traces = inputs
    total_sum = complex_apply(rounded.astype(jnp.float32), map_pair[0].astype(jnp.float32), map_pair[1].astype(jnp.float32)) + drive_traces
    return total_sum.astype(jnp.bfloat16)

def interface_solve(lower_side, upper_side, map_pair, leading):
    leading_flags = leading[:, :, None, None, None]
    ordered = jnp.where(leading_flags == 0, jnp.concatenate([lower_side, upper_side], axis=-1), jnp.concatenate([upper_side, lower_side], axis=-1))
    solved = complex_apply(ordered.astype(jnp.float32), map_pair[:, :, 0].astype(jnp.float32), map_pair[:, :, 1].astype(jnp.float32))
    head_part = solved[..., :FACE]
    tail_part = solved[..., FACE:]
    return (jnp.where(leading_flags == 0, head_part, tail_part), jnp.where(leading_flags == 0, tail_part, head_part))

def reference(sources, impedance, pair_maps, lead_side, coarse_basis, coarse_inverse):
    subdomains = SUB_X * SUB_Y
    iterate = jnp.zeros(sources.shape, jnp.float32)
    flat_maps = impedance.reshape((subdomains,) + impedance.shape[2:])
    flat_drive = sources.reshape((subdomains,) + sources.shape[2:])
    unpadded = (0, 0)
    for repeat in range(ITERS):
        rounded = iterate.astype(jnp.bfloat16).reshape(flat_drive.shape)
        outgoing = lax.map(subdomain_map, (rounded, flat_maps, flat_drive)).reshape(sources.shape)
        first_low, first_high = interface_solve(outgoing[:-1, :, :, :, FACE:2 * FACE], outgoing[1:, :, :, :, :FACE], pair_maps[:-1, :, 0], lead_side[:-1, :, 0])
        second_low, second_high = interface_solve(outgoing[:, :-1, :, :, 3 * FACE:4 * FACE], outgoing[:, 1:, :, :, 2 * FACE:3 * FACE], pair_maps[:, :-1, 1], lead_side[:, :-1, 1])
        face_zero = jnp.pad(first_high, ((1, 0), unpadded, unpadded, unpadded, unpadded))
        face_one = jnp.pad(first_low, ((0, 1), unpadded, unpadded, unpadded, unpadded))
        face_two = jnp.pad(second_high, (unpadded, (1, 0), unpadded, unpadded, unpadded))
        face_three = jnp.pad(second_low, (unpadded, (0, 1), unpadded, unpadded, unpadded))
        updated = jnp.concatenate([face_zero, face_one, face_two, face_three, outgoing[..., 5 * FACE:6 * FACE].astype(jnp.float32), outgoing[..., 4 * FACE:5 * FACE].astype(jnp.float32)], axis=-1)
        defect = updated - iterate
        projected = jnp.einsum('abcsk,abpck->absp', defect, coarse_basis, precision=lax.Precision.HIGHEST)
        gathered = projected.reshape(subdomains, SRC, CPS).transpose(1, 0, 2).reshape(SRC, COARSE)
        coarse = jnp.dot(gathered, coarse_inverse.T, precision=lax.Precision.HIGHEST).reshape(SRC, SUB_X, SUB_Y, CPS)
        correction = jnp.einsum('sabp,abpck->abcsk', coarse, coarse_basis, precision=lax.Precision.HIGHEST)
        defect_norm = lax.optimization_barrier(jnp.sum(defect * defect, axis=(0, 1, 2, 4)))
        correction_norm = lax.optimization_barrier(jnp.sum(correction * correction, axis=(0, 1, 2, 4)))
        factor = STEP_RATIO * jnp.sqrt(defect_norm / (correction_norm + 1e-06))
        iterate = updated + factor[None, None, None, :, None] * correction
    return iterate
```

```python
import jax
import jax.numpy as jnp
from jax import lax
from jax.sharding import PartitionSpec as P

ITERS = 2
STEP_RATIO = 0.4
GRID = ("gx", "gy")
EXACT = lax.Precision.HIGHEST


def shifted(block, axis, distance):
    devices = range(lax.axis_size(axis))
    return lax.ppermute(block, axis, [(i - distance, i) for i in devices if i - distance in devices])


def everyone(block):
    count = lax.axis_size(GRID)
    return lax.all_to_all(jnp.broadcast_to(block[None], (count,) + block.shape), GRID, 0, 0, tiled=True)


def complex_apply(traces, stacked_map):
    rows = traces.shape[-2]
    width = stacked_map.shape[-1] // 2
    flattened = traces.reshape(traces.shape[:-3] + (2 * rows, traces.shape[-1]))
    both = jnp.einsum("...rk,...km->...rm", flattened, stacked_map, preferred_element_type=jnp.float32)
    upper, lower = both[..., :rows, :], both[..., rows:, :]
    return jnp.stack(
        [upper[..., :width] - lower[..., width:], upper[..., width:] + lower[..., :width]], axis=-3
    )


def halves(solver, leading, face_width):
    rows_swapped = jnp.roll(solver, face_width, axis=1)
    head, tail = solver[:, :, :face_width], solver[:, :, face_width:]
    head_s, tail_s = rows_swapped[:, :, :face_width], rows_swapped[:, :, face_width:]
    return jnp.where(leading == 0, head, tail_s), jnp.where(leading == 0, tail, head_s)


def columns(solver):
    return jnp.concatenate([solver[0], solver[1]], axis=-1)


def per_device(sources, impedance, pair_maps, lead_side, coarse_basis, coarse_inverse):
    drive = sources[0, 0]
    sources_here = drive.shape[1]
    face_width = drive.shape[2] // 6
    basis = coarse_basis[0, 0]
    coarse_count = basis.shape[0]
    face = lambda traces, f: traces[..., f * face_width : (f + 1) * face_width]

    own_x, above_x = halves(pair_maps[0, 0, 0], lead_side[0, 0, 0], face_width)
    own_y, above_y = halves(pair_maps[0, 0, 1], lead_side[0, 0, 1], face_width)
    own_x = jnp.where(lax.axis_index("gx") < lax.axis_size("gx") - 1, own_x, jnp.zeros_like(own_x))
    own_y = jnp.where(lax.axis_index("gy") < lax.axis_size("gy") - 1, own_y, jnp.zeros_like(own_y))

    side = lax.axis_index("col")
    other_rows = lax.ppermute(
        coarse_inverse, "col", [(i, i ^ 1) for i in range(lax.axis_size("col"))]
    ) if lax.axis_size("col") == 2 else None
    if other_rows is None:
        rows = lax.all_gather(coarse_inverse, "col", axis=0, tiled=True)
    else:
        rows = jnp.where(
            side == 0,
            jnp.concatenate([coarse_inverse, other_rows]),
            jnp.concatenate([other_rows, coarse_inverse]),
        )
    row_blocks = rows.reshape(coarse_count, -1, coarse_count)

    solvers = None
    iterate = None
    for repeat in range(ITERS):
        if repeat == 0:
            outgoing = drive.astype(jnp.bfloat16)
            x_up = shifted(jnp.concatenate([face(outgoing, 1), above_x], axis=1), "gx", 1)
            y_up = shifted(jnp.concatenate([face(outgoing, 3), above_y], axis=1), "gy", 1)
            x_low, below_x = x_up[:, :sources_here], x_up[:, sources_here:]
            y_low, below_y = y_up[:, :sources_here], y_up[:, sources_here:]
            solvers = jnp.stack([columns(m) for m in (below_x, own_x, below_y, own_y)])
        else:
            rounded = iterate.astype(jnp.bfloat16).reshape(2 * sources_here, -1)
            first = jnp.dot(rounded, impedance[0, 0, 0], preferred_element_type=jnp.float32)
            second = jnp.dot(rounded, impedance[0, 0, 1], preferred_element_type=jnp.float32)
            product = jnp.stack(
                [first[:sources_here] - second[sources_here:], second[:sources_here] + first[sources_here:]]
            )
            outgoing = (product + drive).astype(jnp.bfloat16)
            x_low = shifted(face(outgoing, 1), "gx", 1)
            y_low = shifted(face(outgoing, 3), "gy", 1)
        x_high = shifted(face(outgoing, 0), "gx", -1)
        y_high = shifted(face(outgoing, 2), "gy", -1)
        pairs = jnp.stack(
            [
                jnp.concatenate([x_low, face(outgoing, 0)], axis=-1),
                jnp.concatenate([face(outgoing, 1), x_high], axis=-1),
                jnp.concatenate([y_low, face(outgoing, 2)], axis=-1),
                jnp.concatenate([face(outgoing, 3), y_high], axis=-1),
            ]
        )
        solved = complex_apply(pairs, solvers)
        updated = jnp.concatenate(
            [solved[0], solved[1], solved[2], solved[3],
             face(outgoing, 5).astype(jnp.float32), face(outgoing, 4).astype(jnp.float32)],
            axis=-1,
        )
        defect = updated if iterate is None else updated - iterate
        projected = jnp.einsum("csk,pck->ps", defect, basis, precision=EXACT)
        defect_part = jnp.sum(defect * defect, axis=(0, 2))
        gathered = everyone(jnp.concatenate([projected, jnp.broadcast_to(defect_part, (8, sources_here))]))
        defect_norm = jnp.sum(gathered[:, coarse_count], axis=0)
        coarse = jnp.einsum("nps,qnp->sq", gathered[:, :coarse_count], row_blocks, precision=EXACT)
        correction = jnp.einsum("sp,pck->csk", coarse, basis, precision=EXACT)
        correction_norm = jnp.sum(everyone(jnp.sum(correction * correction, axis=(0, 2))[None]), axis=(0, 1))
        factor = STEP_RATIO * jnp.sqrt(defect_norm / (correction_norm + 1e-06))
        iterate = updated + factor[None, :, None] * correction
    return iterate[None, None]


def solution(mesh):
    return jax.shard_map(
        per_device,
        mesh=mesh,
        in_specs=(
            P("gx", "gy", None, "col", None),
            P("gx", "gy", None, None, None),
            P("gx", "gy", None, None, None, None),
            P("gx", "gy", None),
            P("gx", "gy", None, None, None),
            P(("gx", "gy", "col"), None),
        ),
        out_specs=P("gx", "gy", None, "col", None),
        check_vma=False,
    )
```

```python
import jax
import jax.numpy as jnp
from jax import lax
from jax.sharding import PartitionSpec as P

STEP_RATIO = 0.4
GRID = ("gx", "gy")
EXACT = lax.Precision.HIGHEST


def shifted(block, axis, distance):
    count = lax.axis_size(axis)
    return lax.ppermute(block, axis, [(i, (i + distance) % count) for i in range(count)])


def swap(upward, downward, axis, parity):
    count = lax.axis_size(axis)
    lows = range(parity, count, 2)
    route = [(i, (i + 1) % count) for i in lows] + [((i + 1) % count, i) for i in lows]
    mine = jnp.where(lax.axis_index(axis) % 2 == parity, upward, downward)
    return lax.ppermute(mine, axis, route)


def exchange(upward, downward, axis):
    if lax.axis_size(axis) % 2:
        return shifted(upward, axis, 1), shifted(downward, axis, -1)
    first, second = swap(upward, downward, axis, 0), swap(upward, downward, axis, 1)
    even = lax.axis_index(axis) % 2 == 0
    return jnp.where(even, second, first), jnp.where(even, first, second)


def everyone(block):
    count = lax.axis_size(GRID)
    return lax.all_to_all(jnp.broadcast_to(block[None], (count,) + block.shape), GRID, 0, 0, tiled=True)


def both_halves(rows):
    if lax.axis_size("col") != 2:
        return lax.all_gather(rows, "col", axis=0, tiled=True)
    other = lax.ppermute(rows, "col", [(0, 1), (1, 0)])
    mine_first = lax.axis_index("col") == 0
    return jnp.concatenate([jnp.where(mine_first, rows, other), jnp.where(mine_first, other, rows)])


def complex_apply(traces, stacked_map):
    rows = traces.shape[-2]
    width = stacked_map.shape[-1] // 2
    flattened = traces.reshape(traces.shape[:-3] + (2 * rows, traces.shape[-1]))
    both = jnp.einsum("...rk,...km->...rm", flattened, stacked_map, preferred_element_type=jnp.float32)
    upper, lower = both[..., :rows, :], both[..., rows:, :]
    return jnp.stack(
        [upper[..., :width] - lower[..., width:], upper[..., width:] + lower[..., :width]], axis=-3
    )


def halves(solver, leading, face_width):
    rows_swapped = jnp.roll(solver, face_width, axis=1)
    head, tail = solver[:, :, :face_width], solver[:, :, face_width:]
    head_s, tail_s = rows_swapped[:, :, :face_width], rows_swapped[:, :, face_width:]
    return jnp.where(leading == 0, head, tail_s), jnp.where(leading == 0, tail, head_s)


def columns(solver):
    return jnp.concatenate([solver[0], solver[1]], axis=-1)


def per_device(sources, impedance, pair_maps, lead_side, coarse_basis, coarse_inverse):
    drive = sources[0, 0]
    count = drive.shape[1]
    face_width = drive.shape[2] // 6
    basis = coarse_basis[0, 0]
    coarse_count = basis.shape[0]
    face = lambda traces, f: traces[..., f * face_width : (f + 1) * face_width]

    own_x, above_x = halves(pair_maps[0, 0, 0], lead_side[0, 0, 0], face_width)
    own_y, above_y = halves(pair_maps[0, 0, 1], lead_side[0, 0, 1], face_width)
    inner_x = lax.axis_index("gx") < lax.axis_size("gx") - 1
    inner_y = lax.axis_index("gy") < lax.axis_size("gy") - 1
    own_x, above_x = (jnp.where(inner_x, m, jnp.zeros_like(m)) for m in (own_x, above_x))
    own_y, above_y = (jnp.where(inner_y, m, jnp.zeros_like(m)) for m in (own_y, above_y))

    def joined(parts, outgoing):
        return jnp.concatenate(
            parts + [face(outgoing, 5).astype(jnp.float32), face(outgoing, 4).astype(jnp.float32)], axis=-1
        )

    def project(defect):
        return jnp.einsum("csk,pck->ps", defect, basis, precision=EXACT)

    outgoing = drive.astype(jnp.bfloat16)
    high_y = shifted(face(outgoing, 2), "gy", -1)
    high_x = shifted(face(outgoing, 0), "gx", -1)
    pairs = jnp.stack(
        [jnp.concatenate([face(outgoing, 3), high_y], axis=-1), jnp.concatenate([face(outgoing, 1), high_x], axis=-1)]
    )
    whole = jnp.stack(
        [columns(jnp.concatenate([own_y, above_y], axis=-1)), columns(jnp.concatenate([own_x, above_x], axis=-1))]
    )
    solved = complex_apply(pairs, whole)
    face_two = shifted(solved[0, :, :, face_width:], "gy", 1)
    face_zero = shifted(solved[1, :, :, face_width:], "gx", 1)
    updated = joined([face_zero, solved[1, :, :, :face_width], face_two, solved[0, :, :, :face_width]], outgoing)
    projected = project(updated)
    half = coarse_count // 2
    payload = jnp.concatenate([projected[:half], projected[half:]], axis=1)
    payload, above_y, above_x, part_rows, state, rounded_basis = lax.optimization_barrier(
        (payload, above_y, above_x, coarse_inverse, updated, basis.transpose(1, 0, 2).astype(jnp.bfloat16))
    )
    gathered = everyone(payload)
    below_y, below_x = (
        shifted(jnp.concatenate([m[:, :face_width], m[:, face_width:]], axis=-1), axis, 1)
        for m, axis in ((above_y, "gy"), (above_x, "gx"))
    )
    rows = both_halves(part_rows)
    row_blocks = rows.reshape(coarse_count, -1, coarse_count)

    rounded = jnp.concatenate([state.astype(jnp.bfloat16), rounded_basis], axis=1)
    total = count + coarse_count
    rounded = rounded.reshape(2 * total, -1)
    first = jnp.dot(rounded, impedance[0, 0, 0], preferred_element_type=jnp.float32)
    second = jnp.dot(rounded, impedance[0, 0, 1], preferred_element_type=jnp.float32)
    product = jnp.stack([first[:total] - second[total:], second[:total] + first[total:]])
    defect_part = jnp.sum(updated * updated, axis=(0, 2))

    gathered = jnp.concatenate([gathered[:, :, :count], gathered[:, :, count:]], axis=1)
    coarse = jnp.einsum("nps,qnp->sq", gathered, row_blocks, precision=EXACT)
    correction = jnp.einsum("sp,pck->csk", coarse, basis, precision=EXACT)
    correction_part = jnp.sum(correction * correction, axis=(0, 2))
    response = jnp.einsum("sp,cpk->csk", coarse, product[:, count:], precision=lax.Precision.HIGH)
    outgoing = jnp.concatenate([product[:, :count] + drive, response], axis=1).astype(jnp.bfloat16)
    low_y, high_y = exchange(face(outgoing, 3), face(outgoing, 2), "gy")
    low_x, high_x = exchange(face(outgoing, 1), face(outgoing, 0), "gx")
    below_x, below_y = (
        jnp.concatenate([m[:, :, :face_width], m[:, :, face_width:]], axis=1) for m in (below_x, below_y)
    )
    solvers = jnp.stack([columns(m) for m in (below_x, own_x, below_y, own_y)])
    pairs = jnp.stack(
        [
            jnp.concatenate([low_x, face(outgoing, 0)], axis=-1),
            jnp.concatenate([face(outgoing, 1), high_x], axis=-1),
            jnp.concatenate([low_y, face(outgoing, 2)], axis=-1),
            jnp.concatenate([face(outgoing, 3), high_y], axis=-1),
        ]
    )
    solved = complex_apply(pairs, solvers)
    both = joined([solved[0], solved[1], solved[2], solved[3]], outgoing)
    defects = both - jnp.concatenate([updated, correction], axis=1)
    sums = jnp.concatenate([defect_part, correction_part])
    gathered = everyone(jnp.concatenate([project(defects), jnp.broadcast_to(sums, (8, 2 * count))]))
    totals = jnp.sum(gathered[:, coarse_count], axis=0)
    factor = STEP_RATIO * jnp.sqrt(totals[:count] / (totals[count:] + 1e-06))
    gathered = gathered[:, :coarse_count]
    gathered = gathered[:, :, :count] + factor * gathered[:, :, count:]
    defect = defects[:, :count] + factor[None, :, None] * defects[:, count:]
    updated = both[:, :count] + factor[None, :, None] * both[:, count:]
    coarse = jnp.einsum("nps,qnp->sq", gathered, row_blocks, precision=EXACT)
    correction = jnp.einsum("sp,pck->csk", coarse, basis, precision=EXACT)
    sums = jnp.concatenate([jnp.sum(defect * defect, axis=(0, 2)), jnp.sum(correction * correction, axis=(0, 2))])
    totals = jnp.sum(everyone(sums[None]), axis=(0, 1))
    factor = STEP_RATIO * jnp.sqrt(totals[:count] / (totals[count:] + 1e-06))
    iterate = updated + factor[None, :, None] * correction
    return iterate[None, None]


def solution(mesh):
    return jax.shard_map(
        per_device,
        mesh=mesh,
        in_specs=(
            P("gx", "gy", None, "col", None),
            P("gx", "gy", None, None, None),
            P("gx", "gy", None, None, None, None),
            P("gx", "gy", None),
            P("gx", "gy", None, None, None),
            P(("gx", "gy", "col"), None),
        ),
        out_specs=P("gx", "gy", None, "col", None),
        check_vma=False,
    )
```

```python
import jax
import jax.numpy as jnp
from jax import lax
from jax.experimental import pallas as pl
from jax.experimental.pallas import tpu as pltpu
from jax.sharding import PartitionSpec as P

STEP_RATIO = 0.4
GRID = ("gx", "gy")
EXACT = lax.Precision.HIGHEST


def shifted(block, axis, distance):
    count = lax.axis_size(axis)
    return lax.ppermute(block, axis, [(i, (i + distance) % count) for i in range(count)])


def swap(upward, downward, axis, parity):
    count = lax.axis_size(axis)
    lows = range(parity, count, 2)
    route = [(i, (i + 1) % count) for i in lows] + [((i + 1) % count, i) for i in lows]
    mine = jnp.where(lax.axis_index(axis) % 2 == parity, upward, downward)
    return lax.ppermute(mine, axis, route)


def exchange(upward, downward, axis):
    if lax.axis_size(axis) % 2:
        return shifted(upward, axis, 1), shifted(downward, axis, -1)
    first, second = swap(upward, downward, axis, 0), swap(upward, downward, axis, 1)
    even = lax.axis_index(axis) % 2 == 0
    return jnp.where(even, second, first), jnp.where(even, first, second)


def everyone(block):
    return spread(jnp.broadcast_to(block[None], (lax.axis_size(GRID),) + block.shape))


def spread(copies):
    return lax.all_to_all(copies, GRID, 0, 0, tiled=True)


def both_halves(rows):
    if lax.axis_size("col") != 2:
        return lax.all_gather(rows, "col", axis=0, tiled=True)
    other = lax.ppermute(rows, "col", [(0, 1), (1, 0)])
    mine_first = lax.axis_index("col") == 0
    return jnp.concatenate([jnp.where(mine_first, rows, other), jnp.where(mine_first, other, rows)])


def halves(solver, leading, face_width):
    swapped = jnp.roll(solver, face_width, axis=1)
    lower = jnp.where(leading == 0, solver[:, :, :face_width], swapped[:, :, face_width:])
    upper = jnp.where(leading == 0, solver[:, :, face_width:], swapped[:, :, :face_width])
    return jnp.concatenate([lower[0], lower[1]], axis=-1), jnp.concatenate([upper[0], upper[1]], axis=-1)


def interface_kernel(out, low_x, high_x, low_y, high_y, below_x, own_x, below_y, own_y, first, second, basis, sums,
                     both, payload):
    rows, face_width = low_x.shape[1], low_x.shape[2]
    pair = 2 * face_width
    lane = lax.broadcasted_iota(jnp.int32, (rows, pair), 1)
    is_first = lane < face_width
    turn = lambda value: pltpu.roll(value, face_width, 1)
    dot = lambda a, b: jnp.dot(a, b, preferred_element_type=jnp.float32)
    kept = basis.shape[1] // 2
    projected = jnp.zeros((kept, rows), jnp.float32)
    sides = ((low_x, high_x, below_x, own_x), (low_y, high_y, below_y, own_y), None)
    for block, side in enumerate(sides):
        at = pl.ds(block * pair, pair)
        mine = out[:, :, at]
        if side is None:
            parts = [turn(mine[c].astype(jnp.float32)) for c in range(2)]
        else:
            low, high, below, own = side
            mine = mine.reshape(2 * rows, pair)
            own_rows = jnp.concatenate([jnp.zeros((face_width, pair), own.dtype), own[:face_width]], axis=0)
            below_rows = jnp.concatenate([below[face_width:], jnp.zeros((face_width, pair), own.dtype)], axis=0)
            ahead = dot(low[...].reshape(2 * rows, face_width), below[:face_width]) + dot(mine, below_rows)
            behind = dot(high[...].reshape(2 * rows, face_width), own[face_width:]) + dot(mine, own_rows)
            parts = [
                jnp.where(is_first, ahead[:rows] - turn(ahead[rows:]), turn(behind[:rows]) - behind[rows:]),
                jnp.where(is_first, turn(ahead[:rows]) + ahead[rows:], behind[:rows] + turn(behind[rows:])),
            ]
        for c in range(2):
            both[c, :, at] = parts[c]
            state = jnp.concatenate([first[c, :, at], second[c, :, at]], axis=0)
            defect = parts[c] - state
            coarser = defect.astype(jnp.bfloat16)
            finer = (defect - coarser.astype(jnp.float32)).astype(jnp.bfloat16)
            fit = lambda a, b: lax.dot_general(a, b, (((1,), (1,)), ((), ())), preferred_element_type=jnp.float32)
            main = fit(basis[c, :, at], coarser)
            projected += main[:kept] + main[kept:] + fit(basis[c, :kept, at], finer)
    tail = jnp.broadcast_to(sums[...], (payload.shape[1] - kept, rows))
    for target in range(payload.shape[0]):
        payload[target, :kept] = projected
        payload[target, kept:] = tail


def solve_interfaces(*args):
    out, basis = args[0], args[11]
    rows, width = out.shape[1:]
    full = pl.BlockSpec(memory_space=pltpu.VMEM)
    return pl.pallas_call(
        interface_kernel,
        in_specs=[full] * len(args),
        out_specs=[full, full],
        out_shape=[
            jax.ShapeDtypeStruct((2, rows, width), jnp.float32),
            jax.ShapeDtypeStruct((lax.axis_size(GRID), basis.shape[1] // 2 + 8, rows), jnp.float32),
        ],
        name="interfaces",
        compiler_params=pltpu.CompilerParams(vmem_limit_bytes=12 * 2**20),
        cost_estimate=pl.CostEstimate(flops=24 * rows * width**2 // 9, bytes_accessed=40 * rows * width, transcendentals=0),
    )(*args)


def per_device(sources, impedance, pair_maps, lead_side, coarse_basis, coarse_inverse):
    drive = sources[0, 0]
    count = drive.shape[1]
    face_width = drive.shape[2] // 6
    basis = coarse_basis[0, 0]
    coarse_count = basis.shape[0]
    face = lambda traces, f: traces[..., f * face_width : (f + 1) * face_width]

    inner_x = lax.axis_index("gx") < lax.axis_size("gx") - 1
    inner_y = lax.axis_index("gy") < lax.axis_size("gy") - 1
    basis_first = basis.transpose(1, 0, 2)
    basis_main = basis_first.astype(jnp.bfloat16)
    basis_split = jnp.concatenate(
        [basis_main, (basis_first - lax.reduce_precision(basis_first, 8, 7)).astype(jnp.bfloat16)], axis=1
    )

    def project(defect):
        return jnp.einsum("csk,pck->ps", defect, basis, precision=EXACT)

    out = [face(drive, f).astype(jnp.bfloat16) for f in range(6)]
    high_y = shifted(out[2], "gy", -1)
    high_x = shifted(out[0], "gx", -1)

    def lower_solves(lower, upper, solver, leading, inside):
        stood_first = leading == 0
        ordered = jnp.where(
            stood_first, jnp.concatenate([lower, upper], axis=-1), jnp.concatenate([upper, lower], axis=-1)
        ).reshape(2 * count, -1)
        real, imag = (jnp.dot(ordered, solver[c], preferred_element_type=jnp.float32) for c in range(2))
        solved = jnp.stack([real[:count] - imag[count:], imag[:count] + real[count:]])
        solved = jnp.where(inside, solved, 0.0)
        head, tail = solved[:, :, :face_width], solved[:, :, face_width:]
        return jnp.where(stood_first, head, tail), jnp.where(stood_first, tail, head)

    face_three, up_y = lower_solves(out[3], high_y, pair_maps[0, 0, 1], lead_side[0, 0, 1], inner_y)
    face_one, up_x = lower_solves(out[1], high_x, pair_maps[0, 0, 0], lead_side[0, 0, 0], inner_x)
    up_y, up_x, solvers_here, part_rows = lax.optimization_barrier((up_y, up_x, pair_maps[0, 0], coarse_inverse))
    own_x, above_x = halves(solvers_here[0], lead_side[0, 0, 0], face_width)
    own_y, above_y = halves(solvers_here[1], lead_side[0, 0, 1], face_width)
    own_x, above_x = (jnp.where(inner_x, m, jnp.zeros_like(m)) for m in (own_x, above_x))
    own_y, above_y = (jnp.where(inner_y, m, jnp.zeros_like(m)) for m in (own_y, above_y))
    below_y, below_x = shifted(above_y, "gy", 1), shifted(above_x, "gx", 1)
    face_two = shifted(up_y, "gy", 1)
    face_zero = shifted(up_x, "gx", 1)
    updated = jnp.concatenate(
        [face_zero, face_one, face_two, face_three, out[5].astype(jnp.float32), out[4].astype(jnp.float32)], axis=-1
    )
    projected = project(updated)
    half = coarse_count // 2
    payload = jnp.concatenate([projected[:half], projected[half:]], axis=1)
    payload, state = lax.optimization_barrier((payload, updated))
    gathered = everyone(payload)
    rows = both_halves(part_rows)

    rounded = jnp.concatenate([state, basis_first], axis=1).astype(jnp.bfloat16)
    total = count + coarse_count
    rounded = rounded.reshape(2 * total, -1)
    first = jnp.dot(rounded, impedance[0, 0, 0], preferred_element_type=jnp.float32)
    second = jnp.dot(rounded, impedance[0, 0, 1], preferred_element_type=jnp.float32)
    product = jnp.stack([first[:total] - second[total:], second[:total] + first[total:]])
    defect_part = jnp.sum(updated * updated, axis=(0, 2))

    gathered = jnp.concatenate([gathered[:, :, :count], gathered[:, :, count:]], axis=1)
    coarse = jnp.einsum("qr,rs->qs", rows, gathered.reshape(-1, count), precision=EXACT)
    correction = jnp.einsum("ps,cpk->csk", coarse, basis_first, precision=EXACT)
    correction_part = jnp.sum(correction * correction, axis=(0, 2))
    response = jnp.einsum("ps,cpk->csk", coarse, product[:, count:], precision=lax.Precision.HIGH)
    outgoing = jnp.concatenate([product[:, :count] + drive, response], axis=1).astype(jnp.bfloat16)
    low_y, high_y = exchange(face(outgoing, 3), face(outgoing, 2), "gy")
    low_x, high_x = exchange(face(outgoing, 1), face(outgoing, 0), "gx")
    sums = jnp.concatenate([defect_part, correction_part])[None]
    both, payload = solve_interfaces(
        outgoing, low_x, high_x, low_y, high_y, below_x, own_x, below_y, own_y, updated, correction, basis_split, sums
    )
    gathered = spread(payload)
    totals = jnp.sum(gathered[:, coarse_count], axis=0)
    factor = STEP_RATIO * jnp.sqrt(totals[:count] / (totals[count:] + 1e-06))
    gathered = gathered[:, :coarse_count]
    gathered = gathered[:, :, :count] + factor * gathered[:, :, count:]
    state = updated + factor[None, :, None] * correction
    updated = both[:, :count] + factor[None, :, None] * both[:, count:]
    defect = updated - state
    coarse = jnp.einsum("qr,rs->qs", rows, gathered.reshape(-1, count), precision=EXACT)
    correction = jnp.einsum("ps,cpk->csk", coarse, basis_first, precision=EXACT)
    sums = jnp.concatenate([jnp.sum(defect * defect, axis=(0, 2)), jnp.sum(correction * correction, axis=(0, 2))])
    totals = jnp.sum(everyone(sums[None]), axis=(0, 1))
    factor = STEP_RATIO * jnp.sqrt(totals[:count] / (totals[count:] + 1e-06))
    iterate = updated + factor[None, :, None] * correction
    return iterate[None, None]


def solution(mesh):
    return jax.shard_map(
        per_device,
        mesh=mesh,
        in_specs=(
            P("gx", "gy", None, "col", None),
            P("gx", "gy", None, None, None),
            P("gx", "gy", None, None, None, None),
            P("gx", "gy", None),
            P("gx", "gy", None, None, None),
            P(("gx", "gy", "col"), None),
        ),
        out_specs=P("gx", "gy", None, "col", None),
        check_vma=False,
    )
```

```python
import jax
import jax.numpy as jnp
from jax import lax
from jax.experimental import pallas as pl
from jax.experimental.pallas import tpu as pltpu
from jax.sharding import PartitionSpec as P

STEP_RATIO = 0.4
GRID = ("gx", "gy")
EXACT = lax.Precision.HIGHEST


def shifted(block, axis, distance):
    count = lax.axis_size(axis)
    return lax.ppermute(block, axis, [(i, (i + distance) % count) for i in range(count)])


def swap(upward, downward, axis, parity):
    count = lax.axis_size(axis)
    partner = list(range(count))
    for low in range(parity, count - 1, 2):
        partner[low], partner[low + 1] = low + 1, low
    mine = jnp.where(lax.axis_index(axis) % 2 == parity, upward, downward)
    return lax.ppermute(mine, axis, list(enumerate(partner)))


def exchange(upward, downward, axis):
    first, second = swap(upward, downward, axis, 0), swap(upward, downward, axis, 1)
    even = lax.axis_index(axis) % 2 == 0
    return jnp.where(even, second, first), jnp.where(even, first, second)


def everyone(block):
    return spread(jnp.broadcast_to(block[None], (lax.axis_size(GRID),) + block.shape))


def spread(copies):
    return lax.all_to_all(copies, GRID, 0, 0, tiled=True)


def both_halves(rows):
    if lax.axis_size("col") != 2:
        return lax.all_gather(rows, "col", axis=0, tiled=True)
    other = lax.ppermute(rows, "col", [(0, 1), (1, 0)])
    mine_first = lax.axis_index("col") == 0
    return jnp.concatenate([jnp.where(mine_first, rows, other), jnp.where(mine_first, other, rows)])


def halves(solver, leading, face_width):
    swapped = jnp.roll(solver, face_width, axis=1)
    lower = jnp.where(leading == 0, solver[:, :, :face_width], swapped[:, :, face_width:])
    upper = jnp.where(leading == 0, solver[:, :, face_width:], swapped[:, :, :face_width])
    return jnp.concatenate([lower[0], lower[1]], axis=-1), jnp.concatenate([upper[0], upper[1]], axis=-1)


def interface_kernel(out, low_x, high_x, low_y, high_y, below_x, own_x, below_y, own_y, first, second, basis, sums,
                     both, payload):
    rows, face_width = low_x.shape[1], low_x.shape[2]
    pair = 2 * face_width
    lane = lax.broadcasted_iota(jnp.int32, (rows, pair), 1)
    is_first = lane < face_width
    turn = lambda value: pltpu.roll(value, face_width, 1)
    dot = lambda a, b: jnp.dot(a, b, preferred_element_type=jnp.float32)
    kept = basis.shape[1] // 2
    projected = jnp.zeros((kept, rows), jnp.float32)
    sides = ((low_x, high_x, below_x, own_x), (low_y, high_y, below_y, own_y), None)
    for block, side in enumerate(sides):
        at = pl.ds(block * pair, pair)
        mine = out[:, :, at]
        if side is None:
            parts = [turn(mine[c].astype(jnp.float32)) for c in range(2)]
        else:
            low, high, below, own = side
            mine = mine.reshape(2 * rows, pair)
            own_rows = jnp.concatenate([jnp.zeros((face_width, pair), own.dtype), own[:face_width]], axis=0)
            below_rows = jnp.concatenate([below[face_width:], jnp.zeros((face_width, pair), own.dtype)], axis=0)
            ahead = dot(low[...].reshape(2 * rows, face_width), below[:face_width]) + dot(mine, below_rows)
            behind = dot(high[...].reshape(2 * rows, face_width), own[face_width:]) + dot(mine, own_rows)
            parts = [
                jnp.where(is_first, ahead[:rows] - turn(ahead[rows:]), turn(behind[:rows]) - behind[rows:]),
                jnp.where(is_first, turn(ahead[:rows]) + ahead[rows:], behind[:rows] + turn(behind[rows:])),
            ]
        for c in range(2):
            both[c, :, at] = parts[c]
            state = jnp.concatenate([first[c, :, at], second[c, :, at]], axis=0)
            defect = parts[c] - state
            coarser = defect.astype(jnp.bfloat16)
            finer = (defect - coarser.astype(jnp.float32)).astype(jnp.bfloat16)
            fit = lambda a, b: lax.dot_general(a, b, (((1,), (1,)), ((), ())), preferred_element_type=jnp.float32)
            main = fit(basis[c, :, at], coarser)
            projected += main[:kept] + main[kept:] + fit(basis[c, :kept, at], finer)
    tail = jnp.broadcast_to(sums[...], (payload.shape[1] - kept, rows))
    for target in range(payload.shape[0]):
        payload[target, :kept] = projected
        payload[target, kept:] = tail


def fit(a, b):
    return lax.dot_general(a, b, (((1,), (1,)), ((), ())), preferred_element_type=jnp.float32)


def parted(value):
    coarser = value.astype(jnp.bfloat16)
    return coarser, (value - coarser.astype(jnp.float32)).astype(jnp.bfloat16)


def row_sums(squares):
    coarser, finer = parted(squares)
    ones = jnp.ones((16, squares.shape[1]), jnp.bfloat16)
    return (fit(ones, coarser) + fit(ones, finer))[:1]


def join_kernel(zero, one, two, three, four, five, basis, updated, payload, norms):
    count, face_width = zero.shape[1], zero.shape[2]
    kept, pair = basis.shape[1] // 2, 2 * face_width
    projected = jnp.zeros((kept, 2 * count), jnp.float32)
    squares = jnp.zeros((count, pair), jnp.float32)
    for block, (low, high) in enumerate(((zero, one), (two, three), (five, four))):
        at = pl.ds(block * pair, pair)
        for c in range(2):
            updated[c, :, block * pair : block * pair + face_width] = low[c].astype(jnp.float32)
            updated[c, :, block * pair + face_width : (block + 1) * pair] = high[c].astype(jnp.float32)
            value = updated[c, :, at]
            squares += value * value
            coarser, finer = parted(jnp.concatenate([value, value], axis=0))
            main = fit(basis[c, :, at], coarser)
            projected += main[:kept] + main[kept:] + fit(basis[c, :kept, at], finer)
    norms[...] = row_sums(squares)
    lane = lax.broadcasted_iota(jnp.int32, (kept // 2, 2 * count), 1)
    packed = jnp.where(lane < count, projected[: kept // 2], projected[kept // 2 :])
    for target in range(payload.shape[0]):
        payload[target] = packed


def correct_kernel(gathered, rows, basis, products, drive, norms, correction, outgoing, sums):
    count, kept = drive.shape[1], basis.shape[1]
    total, width = count + kept, drive.shape[2]
    pieces = []
    for n in range(gathered.shape[0]):
        block = gathered[n]
        pieces += [block[:, :count], pltpu.roll(block, count, 1)[:, :count]]
    coarse = jnp.dot(
        rows[...], jnp.concatenate(pieces, axis=0), precision=EXACT, preferred_element_type=jnp.float32
    ).T
    major, minor = parted(coarse)
    weights = jnp.concatenate([major, major, minor], axis=1)

    def combined(vectors):
        upper, lower = parted(vectors)
        return jnp.dot(weights, jnp.concatenate([upper, lower, upper], axis=0), preferred_element_type=jnp.float32)

    squares = jnp.zeros((count, width), jnp.float32)
    for c in range(2):
        value = combined(basis[c])
        correction[c] = value
        squares += value * value
        if c == 0:
            product = products[0, :total] - products[1, total:]
        else:
            product = products[1, :total] + products[0, total:]
        outgoing[c, :count] = (product[:count] + drive[c]).astype(jnp.bfloat16)
        outgoing[c, count:] = combined(product[count:]).astype(jnp.bfloat16)
    sums[...] = jnp.concatenate([norms[...], row_sums(squares)], axis=1)


def on_chip(kernel, out_shape, flops, *args):
    full = pl.BlockSpec(memory_space=pltpu.VMEM)
    moved = sum(a.size * a.dtype.itemsize for a in args)
    return pl.pallas_call(
        kernel,
        in_specs=[full] * len(args),
        out_specs=[full] * len(out_shape),
        out_shape=out_shape,
        compiler_params=pltpu.CompilerParams(vmem_limit_bytes=12 * 2**20),
        cost_estimate=pl.CostEstimate(flops=flops, bytes_accessed=moved, transcendentals=0),
    )(*args)


def solve_interfaces(*args):
    out, basis = args[0], args[11]
    rows, width = out.shape[1:]
    full = pl.BlockSpec(memory_space=pltpu.VMEM)
    return pl.pallas_call(
        interface_kernel,
        in_specs=[full] * len(args),
        out_specs=[full, full],
        out_shape=[
            jax.ShapeDtypeStruct((2, rows, width), jnp.float32),
            jax.ShapeDtypeStruct((lax.axis_size(GRID), basis.shape[1] // 2 + 8, rows), jnp.float32),
        ],
        name="interfaces",
        compiler_params=pltpu.CompilerParams(vmem_limit_bytes=12 * 2**20),
        cost_estimate=pl.CostEstimate(flops=24 * rows * width**2 // 9, bytes_accessed=40 * rows * width, transcendentals=0),
    )(*args)


def per_device(sources, impedance, pair_maps, lead_side, coarse_basis, coarse_inverse):
    drive = sources[0, 0]
    count = drive.shape[1]
    face_width = drive.shape[2] // 6
    basis = coarse_basis[0, 0]
    coarse_count = basis.shape[0]
    face = lambda traces, f: traces[..., f * face_width : (f + 1) * face_width]

    inner_x = lax.axis_index("gx") < lax.axis_size("gx") - 1
    inner_y = lax.axis_index("gy") < lax.axis_size("gy") - 1
    basis_first = basis.transpose(1, 0, 2)
    basis_main = basis_first.astype(jnp.bfloat16)
    basis_split = jnp.concatenate(
        [basis_main, (basis_first - lax.reduce_precision(basis_first, 8, 7)).astype(jnp.bfloat16)], axis=1
    )

    out = [face(drive, f).astype(jnp.bfloat16) for f in range(6)]
    high_y = shifted(out[2], "gy", -1)
    high_x = shifted(out[0], "gx", -1)

    def lower_solves(lower, upper, solver, leading, inside):
        stood_first = leading == 0
        ordered = jnp.where(
            stood_first, jnp.concatenate([lower, upper], axis=-1), jnp.concatenate([upper, lower], axis=-1)
        ).reshape(2 * count, -1)
        real, imag = (jnp.dot(ordered, solver[c], preferred_element_type=jnp.float32) for c in range(2))
        solved = jnp.stack([real[:count] - imag[count:], imag[:count] + real[count:]])
        solved = jnp.where(inside, solved, 0.0)
        head, tail = solved[:, :, :face_width], solved[:, :, face_width:]
        return jnp.where(stood_first, head, tail), jnp.where(stood_first, tail, head)

    face_three, up_y = lower_solves(out[3], high_y, pair_maps[0, 0, 1], lead_side[0, 0, 1], inner_y)
    face_one, up_x = lower_solves(out[1], high_x, pair_maps[0, 0, 0], lead_side[0, 0, 0], inner_x)
    up_y, up_x, solvers_here, part_rows = lax.optimization_barrier((up_y, up_x, pair_maps[0, 0], coarse_inverse))
    own_x, above_x = halves(solvers_here[0], lead_side[0, 0, 0], face_width)
    own_y, above_y = halves(solvers_here[1], lead_side[0, 0, 1], face_width)
    own_x, above_x = (jnp.where(inner_x, m, jnp.zeros_like(m)) for m in (own_x, above_x))
    own_y, above_y = (jnp.where(inner_y, m, jnp.zeros_like(m)) for m in (own_y, above_y))
    below_y, below_x = shifted(above_y, "gy", 1), shifted(above_x, "gx", 1)
    face_two = shifted(up_y, "gy", 1)
    face_zero = shifted(up_x, "gx", 1)
    groups = lax.axis_size(GRID)
    updated, payload, defect_part = on_chip(
        join_kernel,
        [
            jax.ShapeDtypeStruct(drive.shape, jnp.float32),
            jax.ShapeDtypeStruct((groups, coarse_count // 2, 2 * count), jnp.float32),
            jax.ShapeDtypeStruct((1, count), jnp.float32),
        ],
        12 * coarse_count * count * drive.shape[2],
        face_zero, face_one, face_two, face_three, out[4], out[5], basis_split,
    )
    payload, state = lax.optimization_barrier((payload, updated))
    gathered = spread(payload)
    rows = both_halves(part_rows)

    rounded = jnp.concatenate([state, basis_first], axis=1).astype(jnp.bfloat16)
    total = count + coarse_count
    rounded = rounded.reshape(2 * total, -1)
    products = jnp.einsum("rk,ckm->crm", rounded, impedance[0, 0], preferred_element_type=jnp.float32)
    correction, outgoing, sums = on_chip(
        correct_kernel,
        [
            jax.ShapeDtypeStruct(drive.shape, jnp.float32),
            jax.ShapeDtypeStruct((2, 2 * count, drive.shape[2]), jnp.bfloat16),
            jax.ShapeDtypeStruct((1, 2 * count), jnp.float32),
        ],
        24 * coarse_count * count * drive.shape[2],
        gathered, rows, basis_first, products, drive, defect_part,
    )
    low_y, high_y = exchange(face(outgoing, 3), face(outgoing, 2), "gy")
    low_x, high_x = exchange(face(outgoing, 1), face(outgoing, 0), "gx")
    both, payload = solve_interfaces(
        outgoing, low_x, high_x, low_y, high_y, below_x, own_x, below_y, own_y, updated, correction, basis_split, sums
    )
    gathered = spread(payload)
    totals = jnp.sum(gathered[:, coarse_count], axis=0)
    factor = STEP_RATIO * jnp.sqrt(totals[:count] / (totals[count:] + 1e-06))
    gathered = gathered[:, :coarse_count]
    gathered = gathered[:, :, :count] + factor * gathered[:, :, count:]
    state = updated + factor[None, :, None] * correction
    updated = both[:, :count] + factor[None, :, None] * both[:, count:]
    defect = updated - state
    coarse = jnp.einsum("qr,rs->qs", rows, gathered.reshape(-1, count), precision=EXACT)
    correction = jnp.einsum("ps,cpk->csk", coarse, basis_first, precision=EXACT)
    sums = jnp.concatenate([jnp.sum(defect * defect, axis=(0, 2)), jnp.sum(correction * correction, axis=(0, 2))])
    totals = jnp.sum(everyone(sums[None]), axis=(0, 1))
    factor = STEP_RATIO * jnp.sqrt(totals[:count] / (totals[count:] + 1e-06))
    iterate = updated + factor[None, :, None] * correction
    return iterate[None, None]


def solution(mesh):
    return jax.shard_map(
        per_device,
        mesh=mesh,
        in_specs=(
            P("gx", "gy", None, "col", None),
            P("gx", "gy", None, None, None),
            P("gx", "gy", None, None, None, None),
            P("gx", "gy", None),
            P("gx", "gy", None, None, None),
            P(("gx", "gy", "col"), None),
        ),
        out_specs=P("gx", "gy", None, "col", None),
        check_vma=False,
    )
```

```python
import jax
import jax.numpy as jnp
from jax import lax
from jax.experimental import pallas as pl
from jax.experimental.pallas import tpu as pltpu
from jax.sharding import PartitionSpec as P

STEP_RATIO = 0.4
GRID = ("gx", "gy")
EXACT = lax.Precision.HIGHEST


def shifted(block, axis, distance):
    count = lax.axis_size(axis)
    return lax.ppermute(block, axis, [(i, (i + distance) % count) for i in range(count)])


def swap(upward, downward, axis, parity):
    count = lax.axis_size(axis)
    partner = list(range(count))
    for low in range(parity, count - 1, 2):
        partner[low], partner[low + 1] = low + 1, low
    mine = jnp.where(lax.axis_index(axis) % 2 == parity, upward, downward)
    return lax.ppermute(mine, axis, list(enumerate(partner)))


def exchange(upward, downward, axis):
    first, second = swap(upward, downward, axis, 0), swap(upward, downward, axis, 1)
    even = lax.axis_index(axis) % 2 == 0
    return jnp.where(even, second, first), jnp.where(even, first, second)


def everyone(block):
    return spread(jnp.broadcast_to(block[None], (lax.axis_size(GRID),) + block.shape))


def spread(copies):
    return lax.all_to_all(copies, GRID, 0, 0, tiled=True)


def halves_of_rows(rows):
    if lax.axis_size("col") != 2:
        return lax.all_gather(rows, "col", axis=0, tiled=True), None
    return rows, lax.ppermute(rows, "col", [(0, 1), (1, 0)])


def in_order(mine, other):
    if other is None:
        return mine
    mine_first = lax.axis_index("col") == 0
    return jnp.concatenate([jnp.where(mine_first, mine, other), jnp.where(mine_first, other, mine)])


def halves(solver, leading, face_width):
    swapped = jnp.roll(solver, face_width, axis=1)
    lower = jnp.where(leading == 0, solver[:, :, :face_width], swapped[:, :, face_width:])
    upper = jnp.where(leading == 0, solver[:, :, face_width:], swapped[:, :, :face_width])
    return jnp.concatenate([lower[0], lower[1]], axis=-1), jnp.concatenate([upper[0], upper[1]], axis=-1)


def interface_kernel(out, low_x, high_x, low_y, high_y, below_x, own_x, below_y, own_y, first, second, basis, sums,
                     both, payload):
    rows, face_width = low_x.shape[1], low_x.shape[2]
    pair = 2 * face_width
    lane = lax.broadcasted_iota(jnp.int32, (rows, pair), 1)
    is_first = lane < face_width
    turn = lambda value: pltpu.roll(value, face_width, 1)
    dot = lambda a, b: jnp.dot(a, b, preferred_element_type=jnp.float32)
    kept = basis.shape[1] // 2
    projected = jnp.zeros((kept, rows), jnp.float32)
    sides = ((low_x, high_x, below_x, own_x), (low_y, high_y, below_y, own_y), None)
    for block, side in enumerate(sides):
        at = pl.ds(block * pair, pair)
        mine = out[:, :, at]
        if side is None:
            parts = [turn(mine[c].astype(jnp.float32)) for c in range(2)]
        else:
            low, high, below, own = side
            mine = mine.reshape(2 * rows, pair)
            own_rows = jnp.concatenate([jnp.zeros((face_width, pair), own.dtype), own[:face_width]], axis=0)
            below_rows = jnp.concatenate([below[face_width:], jnp.zeros((face_width, pair), own.dtype)], axis=0)
            ahead = dot(low[...].reshape(2 * rows, face_width), below[:face_width]) + dot(mine, below_rows)
            behind = dot(high[...].reshape(2 * rows, face_width), own[face_width:]) + dot(mine, own_rows)
            parts = [
                jnp.where(is_first, ahead[:rows] - turn(ahead[rows:]), turn(behind[:rows]) - behind[rows:]),
                jnp.where(is_first, turn(ahead[:rows]) + ahead[rows:], behind[:rows] + turn(behind[rows:])),
            ]
        for c in range(2):
            both[c, :, at] = parts[c]
            state = jnp.concatenate([first[c, :, at], second[c, :, at]], axis=0)
            defect = parts[c] - state
            coarser = defect.astype(jnp.bfloat16)
            finer = (defect - coarser.astype(jnp.float32)).astype(jnp.bfloat16)
            fit = lambda a, b: lax.dot_general(a, b, (((1,), (1,)), ((), ())), preferred_element_type=jnp.float32)
            main = fit(basis[c, :, at], coarser)
            projected += main[:kept] + main[kept:] + fit(basis[c, :kept, at], finer)
    tail = jnp.broadcast_to(sums[...], (payload.shape[1] - kept, rows))
    for target in range(payload.shape[0]):
        payload[target, :kept] = projected
        payload[target, kept:] = tail


def fit(a, b):
    return lax.dot_general(a, b, (((1,), (1,)), ((), ())), preferred_element_type=jnp.float32)


def parted(value):
    coarser = value.astype(jnp.bfloat16)
    return coarser, (value - coarser.astype(jnp.float32)).astype(jnp.bfloat16)


def row_sums(squares):
    coarser, finer = parted(squares)
    ones = jnp.ones((16, squares.shape[1]), jnp.bfloat16)
    return (fit(ones, coarser) + fit(ones, finer))[:1]


def join_kernel(zero, one, two, three, four, five, basis, updated, payload, norms):
    count, face_width = zero.shape[1], zero.shape[2]
    kept, pair = basis.shape[1] // 2, 2 * face_width
    projected = jnp.zeros((kept, 2 * count), jnp.float32)
    squares = jnp.zeros((count, pair), jnp.float32)
    for block, (low, high) in enumerate(((zero, one), (two, three), (five, four))):
        at = pl.ds(block * pair, pair)
        for c in range(2):
            updated[c, :, block * pair : block * pair + face_width] = low[c].astype(jnp.float32)
            updated[c, :, block * pair + face_width : (block + 1) * pair] = high[c].astype(jnp.float32)
            value = updated[c, :, at]
            squares += value * value
            coarser, finer = parted(jnp.concatenate([value, value], axis=0))
            main = fit(basis[c, :, at], coarser)
            projected += main[:kept] + main[kept:] + fit(basis[c, :kept, at], finer)
    norms[...] = row_sums(squares)
    lane = lax.broadcasted_iota(jnp.int32, (kept // 2, 2 * count), 1)
    packed = jnp.where(lane < count, projected[: kept // 2], projected[kept // 2 :])
    for target in range(payload.shape[0]):
        payload[target] = packed


def correct_kernel(gathered, rows, basis, products, drive, norms, correction, outgoing, sums):
    count, kept = drive.shape[1], basis.shape[1]
    total, width = count + kept, drive.shape[2]
    pieces = []
    for n in range(gathered.shape[0]):
        block = gathered[n]
        pieces += [block[:, :count], pltpu.roll(block, count, 1)[:, :count]]
    coarse = jnp.dot(
        rows[...], jnp.concatenate(pieces, axis=0), precision=EXACT, preferred_element_type=jnp.float32
    ).T
    major, minor = parted(coarse)
    weights = jnp.concatenate([major, major, minor], axis=1)

    def combined(vectors):
        upper, lower = parted(vectors)
        return jnp.dot(weights, jnp.concatenate([upper, lower, upper], axis=0), preferred_element_type=jnp.float32)

    squares = jnp.zeros((count, width), jnp.float32)
    for c in range(2):
        value = combined(basis[c])
        correction[c] = value
        squares += value * value
        if c == 0:
            product = products[0, :total] - products[1, total:]
        else:
            product = products[1, :total] + products[0, total:]
        outgoing[c, :count] = (product[:count] + drive[c]).astype(jnp.bfloat16)
        outgoing[c, count:] = combined(product[count:]).astype(jnp.bfloat16)
    sums[...] = jnp.concatenate([norms[...], row_sums(squares)], axis=1)


def on_chip(kernel, out_shape, flops, *args):
    full = pl.BlockSpec(memory_space=pltpu.VMEM)
    moved = sum(a.size * a.dtype.itemsize for a in args)
    return pl.pallas_call(
        kernel,
        in_specs=[full] * len(args),
        out_specs=[full] * len(out_shape),
        out_shape=out_shape,
        compiler_params=pltpu.CompilerParams(vmem_limit_bytes=12 * 2**20),
        cost_estimate=pl.CostEstimate(flops=flops, bytes_accessed=moved, transcendentals=0),
    )(*args)


def solve_interfaces(*args):
    out, basis = args[0], args[11]
    rows, width = out.shape[1:]
    full = pl.BlockSpec(memory_space=pltpu.VMEM)
    return pl.pallas_call(
        interface_kernel,
        in_specs=[full] * len(args),
        out_specs=[full, full],
        out_shape=[
            jax.ShapeDtypeStruct((2, rows, width), jnp.float32),
            jax.ShapeDtypeStruct((lax.axis_size(GRID), basis.shape[1] // 2 + 8, rows), jnp.float32),
        ],
        name="interfaces",
        compiler_params=pltpu.CompilerParams(vmem_limit_bytes=12 * 2**20),
        cost_estimate=pl.CostEstimate(flops=24 * rows * width**2 // 9, bytes_accessed=40 * rows * width, transcendentals=0),
    )(*args)


def per_device(sources, impedance, pair_maps, lead_side, coarse_basis, coarse_inverse):
    drive = sources[0, 0]
    count = drive.shape[1]
    face_width = drive.shape[2] // 6
    basis = coarse_basis[0, 0]
    coarse_count = basis.shape[0]
    face = lambda traces, f: traces[..., f * face_width : (f + 1) * face_width]

    inner_x = lax.axis_index("gx") < lax.axis_size("gx") - 1
    inner_y = lax.axis_index("gy") < lax.axis_size("gy") - 1
    basis_first = basis.transpose(1, 0, 2)
    basis_main = basis_first.astype(jnp.bfloat16)
    basis_split = jnp.concatenate(
        [basis_main, (basis_first - lax.reduce_precision(basis_first, 8, 7)).astype(jnp.bfloat16)], axis=1
    )

    out = [face(drive, f).astype(jnp.bfloat16) for f in range(6)]
    high_y = shifted(out[2], "gy", -1)
    high_x = shifted(out[0], "gx", -1)

    def lower_solves(lower, upper, solver, leading, inside):
        stood_first = leading == 0
        ordered = jnp.where(
            stood_first, jnp.concatenate([lower, upper], axis=-1), jnp.concatenate([upper, lower], axis=-1)
        ).reshape(2 * count, -1)
        real, imag = (jnp.dot(ordered, solver[c], preferred_element_type=jnp.float32) for c in range(2))
        solved = jnp.stack([real[:count] - imag[count:], imag[:count] + real[count:]])
        solved = jnp.where(inside, solved, 0.0)
        head, tail = solved[:, :, :face_width], solved[:, :, face_width:]
        return jnp.where(stood_first, head, tail), jnp.where(stood_first, tail, head)

    face_three, up_y = lower_solves(out[3], high_y, pair_maps[0, 0, 1], lead_side[0, 0, 1], inner_y)
    face_one, up_x = lower_solves(out[1], high_x, pair_maps[0, 0, 0], lead_side[0, 0, 0], inner_x)
    up_y, up_x, solvers_here, part_rows = lax.optimization_barrier((up_y, up_x, pair_maps[0, 0], coarse_inverse))
    own_x, above_x = halves(solvers_here[0], lead_side[0, 0, 0], face_width)
    own_y, above_y = halves(solvers_here[1], lead_side[0, 0, 1], face_width)
    own_x, above_x = (jnp.where(inner_x, m, jnp.zeros_like(m)) for m in (own_x, above_x))
    own_y, above_y = (jnp.where(inner_y, m, jnp.zeros_like(m)) for m in (own_y, above_y))
    below_y, below_x = shifted(above_y, "gy", 1), shifted(above_x, "gx", 1)
    face_two = shifted(up_y, "gy", 1)
    face_zero = shifted(up_x, "gx", 1)
    groups = lax.axis_size(GRID)
    updated, payload, defect_part = on_chip(
        join_kernel,
        [
            jax.ShapeDtypeStruct(drive.shape, jnp.float32),
            jax.ShapeDtypeStruct((groups, coarse_count // 2, 2 * count), jnp.float32),
            jax.ShapeDtypeStruct((1, count), jnp.float32),
        ],
        12 * coarse_count * count * drive.shape[2],
        face_zero, face_one, face_two, face_three, out[4], out[5], basis_split,
    )
    payload, state = lax.optimization_barrier((payload, updated))
    gathered = spread(payload)
    mine, other = halves_of_rows(part_rows)

    rounded = jnp.concatenate([state, basis_first], axis=1).astype(jnp.bfloat16)
    total = count + coarse_count
    rounded = rounded.reshape(2 * total, -1)
    products = jnp.einsum("rk,ckm->crm", rounded, impedance[0, 0], preferred_element_type=jnp.float32)
    products, mine, other = lax.optimization_barrier((products, mine, other))
    rows = in_order(mine, other)
    correction, outgoing, sums = on_chip(
        correct_kernel,
        [
            jax.ShapeDtypeStruct(drive.shape, jnp.float32),
            jax.ShapeDtypeStruct((2, 2 * count, drive.shape[2]), jnp.bfloat16),
            jax.ShapeDtypeStruct((1, 2 * count), jnp.float32),
        ],
        24 * coarse_count * count * drive.shape[2],
        gathered, rows, basis_first, products, drive, defect_part,
    )
    low_y, high_y = exchange(face(outgoing, 3), face(outgoing, 2), "gy")
    low_x, high_x = exchange(face(outgoing, 1), face(outgoing, 0), "gx")
    both, payload = solve_interfaces(
        outgoing, low_x, high_x, low_y, high_y, below_x, own_x, below_y, own_y, updated, correction, basis_split, sums
    )
    gathered = spread(payload)
    totals = jnp.sum(gathered[:, coarse_count], axis=0)
    factor = STEP_RATIO * jnp.sqrt(totals[:count] / (totals[count:] + 1e-06))
    gathered = gathered[:, :coarse_count]
    gathered = gathered[:, :, :count] + factor * gathered[:, :, count:]
    state = updated + factor[None, :, None] * correction
    updated = both[:, :count] + factor[None, :, None] * both[:, count:]
    defect = updated - state
    coarse = jnp.einsum("qr,rs->qs", rows, gathered.reshape(-1, count), precision=EXACT)
    correction = jnp.einsum("ps,cpk->csk", coarse, basis_first, precision=EXACT)
    sums = jnp.concatenate([jnp.sum(defect * defect, axis=(0, 2)), jnp.sum(correction * correction, axis=(0, 2))])
    totals = jnp.sum(everyone(sums[None]), axis=(0, 1))
    factor = STEP_RATIO * jnp.sqrt(totals[:count] / (totals[count:] + 1e-06))
    iterate = updated + factor[None, :, None] * correction
    return iterate[None, None]


def solution(mesh):
    return jax.shard_map(
        per_device,
        mesh=mesh,
        in_specs=(
            P("gx", "gy", None, "col", None),
            P("gx", "gy", None, None, None),
            P("gx", "gy", None, None, None, None),
            P("gx", "gy", None),
            P("gx", "gy", None, None, None),
            P(("gx", "gy", "col"), None),
        ),
        out_specs=P("gx", "gy", None, "col", None),
        check_vma=False,
    )
```
